32 devices in a mesh: dp: 4 (over y, x), tensor: 8 (over z, core).
Axes of the slice: x: 2, y: 2, z: 4, core: 2. Of those that a mesh axis runs over, the one named last changes fastest.
Arguments:
- saved_inputs: bfloat16 [1536, 6144], P(('dp', 'tensor')), may hold values from -6 to 6
- hidden_grads: bfloat16 [1536, 24576], P('dp', 'tensor'), may hold values from -6 to 6
- up_weight: bfloat16 [6144, 24576], P(None, 'tensor'), may hold values from -0.078125 to 0.078125
- up_bias: float32 [24576], P('tensor'), may hold values from -1 to 1
Outputs:
- input_grads: bfloat16 [1536, 6144], P(('dp', 'tensor'))
- weight_grads: bfloat16 [6144, 24576], P('dp', 'tensor')
The draws below stay inside these ranges and needn't reach their ends.
All inputs are finite; a program needn't handle non-finite values.
Results may differ from the reference program's by a relative error of at most 0.014.
Values may be sent and summed in bfloat16 or wider, within the bound.
No kernel may reach another device: no remote copies, remote signals or barrier semaphores. Data moves between devices by JAX's collectives and lax.ppermute only.
A program may use at most 192 MiB of HBM per device.

```python
import jax
import jax.numpy as jnp
from jax import lax

D = 6144
FF = 24576
TOK_DEV = 384
TOKENS = 1536
N_DP = 4


def spiked(result, own_key, source, target, blocks, factor):
    def block_of(position):
        return (jnp.arange(result.shape[position]) // (result.shape[position] // blocks)).reshape((-1,) + (1,) * (result.ndim - 1 - position))

    near = jax.random.permutation(own_key, blocks)[block_of(target)]
    far = (block_of(target) + blocks // 2) % blocks
    return jnp.where((block_of(source) == near) | (block_of(source) == far), factor * result, result)


def levels(stream_key, dims, cuts, smallest, top_value):
    gain = 1.0
    for position, shards_of in cuts:
        steps = jax.random.uniform(jax.random.fold_in(jax.random.fold_in(stream_key, 6), position), (shards_of,), jnp.float32, smallest / len(cuts), top_value / len(cuts))
        gain = gain * jnp.repeat(jnp.exp(steps), dims[position] // shards_of).reshape((-1,) + (1,) * (len(dims) - 1 - position))
    return gain


def centred(rng, shape, deviation, limit, cuts=(), held_as=jnp.bfloat16):
    loudness = levels(rng, shape, cuts, -0.22, 0.18) if cuts else 1.0
    values = jax.random.normal(rng, shape, jnp.float32) * deviation * loudness
    return jnp.minimum(jnp.maximum(values, -limit), limit).astype(held_as)


def heavy_noise(key, dims, width, bound, cuts, heavy, kind=jnp.bfloat16):
    drawn = width * jax.random.normal(key, dims, jnp.float32)
    if cuts:
        drawn = drawn * levels(key, dims, cuts, -0.22, 0.18)
    return jnp.clip(spiked(drawn, jax.random.fold_in(key, 3), *heavy), -bound, bound).astype(kind)


def setup_inputs(seed: int = 0) -> dict:
    arg_keys = jax.random.split(jax.random.key(seed), 5)
    saved_inputs = heavy_noise(arg_keys[0], (TOKENS, D), 1.0, 6.0, ((0, 32),), (0, 1, 32, 2.75))
    hidden_grads = centred(arg_keys[1], (TOKENS, FF), 1.0, 6.0, ((0, 4), (1, 8)))
    up_weight = centred(arg_keys[2], (D, FF), D ** -0.5, 0.078125, ((1, 8),))
    up_bias = jnp.clip(jax.random.uniform(arg_keys[3], (FF,), jnp.float32, -1.0, 1.0) * levels(arg_keys[3], (FF,), ((0, 8),), -0.4, 0.0), -1.0, 1.0)
    return dict(saved_inputs=saved_inputs, hidden_grads=hidden_grads, up_weight=up_weight, up_bias=up_bias)


def slope(pre):
    cdf = 0.5 * (1.0 + jax.scipy.special.erf(pre * 0.7071067811865476))
    pdf = jnp.exp(-0.5 * pre * pre) * 0.3989422804014327
    return cdf + pre * pdf

def reference(saved_inputs, hidden_grads, up_weight, up_bias):
    pre = jnp.dot(saved_inputs, up_weight, preferred_element_type=jnp.float32) + up_bias.astype(jnp.float32)
    local_grads = (hidden_grads.astype(jnp.float32) * slope(pre)).astype(jnp.bfloat16)
    input_grads = lax.dot_general(local_grads, up_weight, (((1,), (1,)), ((), ())), preferred_element_type=jnp.float32).astype(jnp.bfloat16)
    inputs_rep = saved_inputs.reshape(N_DP, TOK_DEV, D)
    grads_rep = local_grads.reshape(N_DP, TOK_DEV, FF)

    def add_replica(total, pair):
        part = lax.dot_general(pair[0], pair[1], (((0,), (0,)), ((), ())), preferred_element_type=jnp.float32)
        rounded = lax.optimization_barrier(part.astype(jnp.bfloat16))
        return (total + rounded.astype(jnp.float32), None)
    summed, _ = lax.scan(add_replica, jnp.zeros((D, FF), jnp.float32), (inputs_rep, grads_rep))
    weight_grads = (summed * (1.0 / jnp.sqrt(jnp.float32(TOKENS)))).astype(jnp.bfloat16)
    return (input_grads, weight_grads)
```

```python
import jax
import jax.numpy as jnp
from jax import lax
from jax.experimental import pallas as pl
from jax.experimental.pallas import tpu as pltpu
from jax.sharding import PartitionSpec as P

VMEM_BYTES = 60 * 1024 * 1024
HALVES = 2


def slope(pre):
    cdf = 0.5 * (1.0 + lax.erf(pre * 0.7071067811865476))
    pdf = jnp.exp(-0.5 * pre * pre) * 0.3989422804014327
    return cdf + pre * pdf


def tile_of(size, most):
    for tile in (1024, 768, 512, 384, 256, 128):
        if tile <= most and size % tile == 0:
            return tile
    return size


def params():
    return pltpu.CompilerParams(vmem_limit_bytes=VMEM_BYTES)


def cost(flops, nbytes, trans=0):
    return pl.CostEstimate(flops=flops, bytes_accessed=nbytes, transcendentals=trans)


def grads_of(x, hidden, weight, bias, half):
    rows, depth = x.shape
    width = weight.shape[1] // HALVES
    bn = tile_of(width, 512)
    steps = width // bn

    def kernel(x_ref, h_ref, w_ref, b_ref, o_ref):
        pre = jnp.dot(x_ref[...], w_ref[...], preferred_element_type=jnp.float32) + b_ref[...]
        o_ref[...] = (h_ref[...].astype(jnp.float32) * slope(pre)).astype(jnp.bfloat16)

    return pl.pallas_call(
        kernel,
        grid=(steps,),
        name="grads_of",
        in_specs=[
            pl.BlockSpec((rows, depth), lambda j: (0, 0)),
            pl.BlockSpec((rows, bn), lambda j: (0, j + half * steps)),
            pl.BlockSpec((depth, bn), lambda j: (0, j + half * steps)),
            pl.BlockSpec((1, bn), lambda j: (0, j + half * steps)),
        ],
        out_specs=pl.BlockSpec((rows, bn), lambda j: (0, j)),
        out_shape=jax.ShapeDtypeStruct((rows, width), jnp.bfloat16),
        compiler_params=params(),
        cost_estimate=cost(2 * rows * depth * width, 2 * depth * width, rows * width),
    )(x, hidden, weight, bias)


def inputs_part(groups, weight, part, parts):
    count = len(groups)
    rows, width = groups[0][0].shape
    depth, full = weight.shape
    cols = depth // parts
    bd = tile_of(cols, 512)
    steps = cols // bd
    own = rows // 2

    def kernel(*refs):
        lg_refs, (w_ref, keep_ref, send_ref, lhs) = refs[: count * HALVES], refs[count * HALVES :]

        @pl.when(pl.program_id(0) == 0)
        def _():
            for g in range(count):
                for h in range(HALVES):
                    lhs[g * rows : (g + 1) * rows, h * width : (h + 1) * width] = lg_refs[g * HALVES + h][...]

        out = lax.dot_general(
            lhs[...], w_ref[...], (((1,), (1,)), ((), ())), preferred_element_type=jnp.float32
        ).astype(jnp.bfloat16)
        for g in range(count):
            keep_ref[g] = out[g * rows : g * rows + own]
            send_ref[g] = out[g * rows + own : (g + 1) * rows]

    flat = [a for group in groups for a in group]
    shape = jax.ShapeDtypeStruct((count, own, cols), jnp.bfloat16)
    return pl.pallas_call(
        kernel,
        grid=(steps,),
        name="inputs_part",
        in_specs=[pl.BlockSpec((rows, width), lambda j: (0, 0)) for _ in flat]
        + [pl.BlockSpec((bd, full), lambda j: (j + part * steps, 0))],
        out_specs=[pl.BlockSpec((count, own, bd), lambda j: (0, 0, j))] * 2,
        out_shape=[shape, shape],
        scratch_shapes=[pltpu.VMEM((count * rows, full), jnp.bfloat16)],
        compiler_params=params(),
        cost_estimate=cost(2 * count * rows * full * cols, 2 * full * cols),
    )(*flat, weight)


def weights_part(xt, pieces, buffers, factor, half, full, out):
    tokens, rows = xt.shape
    width = buffers[0].shape[-1]
    bn = tile_of(width, 512)
    steps = width // bn
    n = len(buffers)

    def kernel(x_ref, *refs):
        lg_refs, o_ref = refs[:n], refs[-1]
        rhs = jnp.concatenate([lg_refs[b][i] for b, i in pieces], axis=0)
        acc = lax.dot_general(
            x_ref[...], rhs, (((0,), (0,)), ((), ())), preferred_element_type=jnp.float32
        )
        o_ref[...] = (acc * factor).astype(jnp.bfloat16)

    extra = [] if out is None else [out]
    return pl.pallas_call(
        kernel,
        grid=(steps,),
        name="weights_part",
        in_specs=[pl.BlockSpec((tokens, rows), lambda j: (0, 0))]
        + [pl.BlockSpec(b.shape[:2] + (bn,), lambda j: (0, 0, j)) for b in buffers]
        + [pl.BlockSpec(memory_space=pl.ANY) for _ in extra],
        out_specs=pl.BlockSpec((rows, bn), lambda j: (0, j + half * steps)),
        out_shape=jax.ShapeDtypeStruct((rows, full), jnp.bfloat16),
        input_output_aliases={1 + n: 0} if extra else {},
        compiler_params=params(),
        cost_estimate=cost(2 * tokens * rows * width, 2 * (tokens * rows + tokens * width + rows * width)),
    )(xt, *buffers, *extra)


def swap(value, axis, bit):
    n = lax.axis_size(axis)
    return lax.ppermute(value, axis, [(i, i ^ bit) for i in range(n)])


def bits_of(n):
    out, b = [], 1
    while b < n:
        out.append(b)
        b *= 2
    return out


def widen(value, bits):
    for b in bits:
        value = jnp.concatenate([value, swap(value, "tensor", b)], axis=0)
    return value


def spread(value, bits):
    cur, rel = value[None], [0]
    got, got_rel = None, None
    for k, b in enumerate(bits):
        if k:
            cur, rel = jnp.concatenate([cur, got], axis=0), rel + got_rel
        got = swap(cur, "dp", b)
        got_rel = [r ^ b for r in rel]
    return [(cur, rel), (got, got_rel)]


def to_owner(x, bits):
    me = lax.axis_index("dp")
    cur, rel = x[None], [0]
    for b in reversed(bits):
        half = cur.shape[2] // 2
        mine = (me // b) % 2
        send = lax.dynamic_slice_in_dim(cur, (1 - mine) * half, half, 2)
        keep = lax.dynamic_slice_in_dim(cur, mine * half, half, 2)
        cur = jnp.concatenate([keep, swap(send, "dp", b)], axis=0)
        rel = rel + [r ^ b for r in rel]
    return cur, rel


def add(a, b):
    return (a.astype(jnp.float32) + b.astype(jnp.float32)).astype(jnp.bfloat16)


def body(saved_inputs, hidden_grads, up_weight, up_bias):
    ranks = lax.axis_size("tensor")
    replicas = lax.axis_size("dp")
    me = lax.axis_index("tensor")
    shard, depth = saved_inputs.shape
    full = up_weight.shape[1]
    tokens = hidden_grads.shape[0] * replicas
    factor = float(1.0 / (tokens**0.5))
    bits = bits_of(ranks)
    top, middle = bits[-1], bits[1:-1]
    dp_bits = bits_of(replicas)
    bias = up_bias.reshape(1, full)

    far = swap(saved_inputs, "tensor", top)
    own = [widen(saved_inputs, middle), widen(far, middle)]
    both = [jnp.concatenate([o, swap(o, "tensor", 1)], axis=0) for o in own]

    order = [0]
    for b in middle:
        order = order + [r ^ b for r in order]
    hidden = []
    for side in (0, top):
        rel = [c ^ r ^ side for c in (0, 1) for r in order]
        hidden.append(
            jnp.concatenate(
                [lax.dynamic_slice_in_dim(hidden_grads, (me ^ r) * shard, shard, 0) for r in rel], axis=0
            )
        )

    orders = [dp_bits, dp_bits[::-1]]
    groups, spreads = [], []
    for g in range(2):
        local = [grads_of(both[g], hidden[g], up_weight, bias, h) for h in range(HALVES)]
        groups.append(local)
        spreads.append([spread(local[h], orders[h % 2]) for h in range(HALVES)])

    moved = [to_owner(o, dp_bits) for o in own]
    rel_rows = moved[0][1]
    xt = jnp.stack(
        [jnp.stack([m, swap(m, "tensor", 1)], axis=1) for m, _ in moved], axis=1
    ).reshape(tokens, depth // replicas)

    parts = []
    for part in range(2):
        keep, send = inputs_part(groups, up_weight, part, 2)
        cur = add(keep, swap(send, "tensor", 1))
        for b in reversed(middle):
            n = cur.shape[1] // 2
            cur = add(cur[:, :n], swap(cur[:, n:], "tensor", b))
        parts.append(add(cur[0], swap(cur[1], "tensor", top)))
    input_grads = jnp.concatenate(parts, axis=1)

    out = None
    for h in range(HALVES):
        buffers, where = [], {}
        for g in range(2):
            for buf, rel in spreads[g][h]:
                for i, r in enumerate(rel):
                    where[g, r] = (len(buffers), i)
                buffers.append(buf)
        pieces = [where[g, r] for r in rel_rows for g in range(2)]
        out = weights_part(xt, pieces, buffers, factor, h, full, out)
    return (input_grads, out)


def solution(mesh):
    return jax.shard_map(
        body,
        mesh=mesh,
        in_specs=(P(("dp", "tensor"), None), P("dp", "tensor"), P(None, "tensor"), P("tensor")),
        out_specs=(P(("dp", "tensor"), None), P("dp", "tensor")),
        check_vma=False,
    )
```

```python
import math

import jax
import jax.numpy as jnp
from jax import lax
from jax.experimental import pallas as pl
from jax.experimental.pallas import tpu as pltpu
from jax.sharding import PartitionSpec as P


VMEM_BYTES = 32 * 1024 * 1024


def slope(pre):
    cdf = 0.5 * (1.0 + lax.erf(pre * 0.7071067811865476))
    pdf = jnp.exp(-0.5 * pre * pre) * 0.3989422804014327
    return cdf + pre * pdf


def tile_of(size, most):
    for tile in (1024, 768, 512, 384, 256, 128):
        if tile <= most and size % tile == 0:
            return tile
    return size


def params():
    return pltpu.CompilerParams(vmem_limit_bytes=VMEM_BYTES)


def cost(flops, nbytes, trans=0):
    return pl.CostEstimate(flops=flops, bytes_accessed=nbytes, transcendentals=trans)


def resident(shape):
    return pl.BlockSpec(shape, lambda j, *_: (0,) * len(shape))


def grads_of(parts, hidden, weight, bias, part, count):
    depth = parts[0].shape[1]
    rows = sum(p.shape[0] for p in parts)
    width = weight.shape[1] // count
    bn = tile_of(width, 512)
    steps = width // bn
    n = len(parts)

    def kernel(*refs):
        x_refs, (h_ref, w_ref, b_ref, o_ref, lhs) = refs[:n], refs[n:]

        @pl.when(pl.program_id(0) == 0)
        def _():
            at = 0
            for ref in x_refs:
                lhs[at : at + ref.shape[0]] = ref[...]
                at += ref.shape[0]

        pre = jnp.dot(lhs[...], w_ref[...], preferred_element_type=jnp.float32) + b_ref[...]
        o_ref[...] = (h_ref[...].astype(jnp.float32) * slope(pre)).astype(jnp.bfloat16)

    return pl.pallas_call(
        kernel,
        grid=(steps,),
        in_specs=[resident(p.shape) for p in parts]
        + [
            pl.BlockSpec((rows, bn), lambda j: (0, j + part * steps)),
            pl.BlockSpec((depth, bn), lambda j: (0, j + part * steps)),
            pl.BlockSpec((1, bn), lambda j: (0, j + part * steps)),
        ],
        out_specs=pl.BlockSpec((rows, bn), lambda j: (0, j)),
        out_shape=jax.ShapeDtypeStruct((rows, width), jnp.bfloat16),
        scratch_shapes=[pltpu.VMEM((rows, depth), jnp.bfloat16)],
        compiler_params=params(),
        cost_estimate=cost(2 * rows * depth * width, 2 * depth * width, rows * width),
    )(*parts, hidden, weight, bias)


def inputs_part(groups, weight, start, cols):
    count = len(groups)
    rows = groups[0][0].shape[0]
    _, full = weight.shape
    bd = tile_of(math.gcd(start, cols), 1024)
    steps = cols // bd
    own = rows // 2
    flat = [a for group in groups for a in group]
    n = len(flat)

    def kernel(*refs):
        lg_refs, (w_ref, keep_ref, send_ref, lhs) = refs[:n], refs[n:]

        @pl.when(pl.program_id(0) == 0)
        def _():
            k = 0
            for g in range(count):
                at = 0
                for a in groups[g]:
                    lhs[g * rows : (g + 1) * rows, at : at + a.shape[1]] = lg_refs[k][...]
                    at += a.shape[1]
                    k += 1

        out = lax.dot_general(
            lhs[...], w_ref[...], (((1,), (1,)), ((), ())), preferred_element_type=jnp.float32
        ).astype(jnp.bfloat16)
        for g in range(count):
            keep_ref[g] = out[g * rows : g * rows + own]
            send_ref[g] = out[g * rows + own : (g + 1) * rows]

    shape = jax.ShapeDtypeStruct((count, own, cols), jnp.bfloat16)
    return pl.pallas_call(
        kernel,
        grid=(steps,),
        in_specs=[resident(a.shape) for a in flat]
        + [pl.BlockSpec((bd, full), lambda j: (j + start // bd, 0))],
        out_specs=[pl.BlockSpec((count, own, bd), lambda j: (0, 0, j))] * 2,
        out_shape=[shape, shape],
        scratch_shapes=[pltpu.VMEM((count * rows, full), jnp.bfloat16)],
        compiler_params=params(),
        cost_estimate=cost(2 * count * rows * full * cols, 2 * full * cols),
    )(*flat, weight)


def gather_rows(spot, sources, pieces):
    tokens = sum(p[2] for p in pieces)
    cols = min(s.shape[1] for s in sources)
    m = len(sources)

    def kernel(spot_ref, *refs):
        src_refs, (o_ref, sem) = refs[:m], refs[m:]
        copies, at = [], 0
        for k, (s, row, size, pick) in enumerate(pieces):
            col = pl.multiple_of(spot_ref[0] * cols, 128) if pick else 0
            copies.append(
                pltpu.make_async_copy(
                    src_refs[s].at[pl.ds(row, size), pl.ds(col, cols)],
                    o_ref.at[pl.ds(at, size), :],
                    sem.at[k],
                )
            )
            at += size
        for c in copies:
            c.start()
        for c in copies:
            c.wait()

    return pl.pallas_call(
        kernel,
        grid_spec=pltpu.PrefetchScalarGridSpec(
            num_scalar_prefetch=1,
            grid=(1,),
            in_specs=[pl.BlockSpec(memory_space=pl.ANY) for _ in sources],
            out_specs=pl.BlockSpec((tokens, cols), lambda j, _: (0, 0)),
            scratch_shapes=[pltpu.SemaphoreType.DMA((len(pieces),))],
        ),
        out_shape=jax.ShapeDtypeStruct((tokens, cols), jnp.bfloat16),
        compiler_params=pltpu.CompilerParams(vmem_limit_bytes=VMEM_BYTES // 2),
        cost_estimate=cost(0, 4 * tokens * cols),
    )(spot, *sources)


def weights_of(xt, buffers, pieces, factor):
    tokens, rows = xt.shape
    full = buffers[0].shape[1]
    bn = tile_of(full, 512)
    n = len(buffers)

    def kernel(x_ref, *refs):
        lg_refs, o_ref = refs[:n], refs[n]
        rhs = jnp.concatenate([lg_refs[b][row : row + size] for b, row, size in pieces], axis=0)
        acc = lax.dot_general(x_ref[...], rhs, (((0,), (0,)), ((), ())), preferred_element_type=jnp.float32)
        o_ref[...] = (acc * factor).astype(jnp.bfloat16)

    return pl.pallas_call(
        kernel,
        grid=(full // bn,),
        in_specs=[resident(xt.shape)] + [pl.BlockSpec((b.shape[0], bn), lambda j: (0, j)) for b in buffers],
        out_specs=pl.BlockSpec((rows, bn), lambda j: (0, j)),
        out_shape=jax.ShapeDtypeStruct((rows, full), jnp.bfloat16),
        compiler_params=params(),
        cost_estimate=cost(2 * tokens * rows * full, 2 * rows * full),
    )(xt, *buffers)


def swap(value, axis, bit):
    n = lax.axis_size(axis)
    return lax.ppermute(value, axis, [(i, i ^ bit) for i in range(n)])


def bits_of(n):
    out, b = [], 1
    while b < n:
        out.append(b)
        b *= 2
    return out


def widen(value, bits):
    for b in bits:
        value = jnp.concatenate([value, swap(value, "tensor", b)], axis=0)
    return value


def collect(value, bits):
    values = [value]
    for b in bits:
        values = values + [swap(v, "tensor", b) for v in values]
    return values


def spread(name, value, bits):
    rows = value.shape[0]
    if len(bits) == 2:
        first, second = bits
        a = swap(value, "dp", first)
        b = swap(value, "dp", second)
        tail = swap(a, "dp", second) if name == "a" else swap(b, "dp", first)
        return [value, a, b, tail], {
            0: [(0, 0, rows)],
            first: [(1, 0, rows)],
            second: [(2, 0, rows)],
            first ^ second: [(3, 0, rows)],
        }
    cur, rel = value, [0]
    got, got_rel = None, []
    for k, b in enumerate(bits):
        if k:
            cur, rel = jnp.concatenate([cur, got], axis=0), rel + got_rel
        got = swap(cur, "dp", b)
        got_rel = [r ^ b for r in rel]
    where = {r: [(0, i * rows, rows)] for i, r in enumerate(rel)}
    where.update({r: [(1, i * rows, rows)] for i, r in enumerate(got_rel)})
    return [cur, got], where


def to_owner(x, bits):
    me = lax.axis_index("dp")
    cur, rel = x[None], [0]
    for b in reversed(bits):
        half = cur.shape[2] // 2
        mine = (me // b) % 2
        send = lax.dynamic_slice_in_dim(cur, (1 - mine) * half, half, 2)
        keep = lax.dynamic_slice_in_dim(cur, mine * half, half, 2)
        cur = jnp.concatenate([keep, swap(send, "dp", b)], axis=0)
        rel = rel + [r ^ b for r in rel]
    return cur[1:].reshape(-1, cur.shape[2]), rel[1:]


def add(a, b):
    return (a.astype(jnp.float32) + b.astype(jnp.float32)).astype(jnp.bfloat16)


def body(saved_inputs, hidden_grads, up_weight, up_bias):
    ranks = lax.axis_size("tensor")
    replicas = lax.axis_size("dp")
    me = lax.axis_index("tensor")
    spot = lax.axis_index("dp").astype(jnp.int32).reshape(1)
    shard, depth = saved_inputs.shape
    full = up_weight.shape[1]
    tokens = hidden_grads.shape[0] * replicas
    factor = float(1.0 / (tokens**0.5))
    bits = bits_of(ranks)
    top, middle = bits[-1], bits[1:-1]
    dp_bits = bits_of(replicas)
    bias = up_bias.reshape(1, full)

    order = [0]
    for b in middle:
        order = order + [r ^ b for r in order]
    hidden = []
    for side in (0, top):
        rel = [c ^ r ^ side for c in (0, 1) for r in order]
        hidden.append(
            jnp.concatenate([lax.dynamic_slice_in_dim(hidden_grads, (me ^ r) * shard, shard, 0) for r in rel], axis=0)
        )

    moved, moved_rel = to_owner(saved_inputs, dp_bits)
    if len(middle) == 1:
        ends, inner, out_of = [], [], []
        for z, core in ((z, c) for z in range(4) for c in (0, 1)):
            here = 2 * z + core
            if z in (1, 2):
                inner.append((here, 2 * (3 - z) + core))
                out_of.append((here, 2 * (3 * (z - 1)) + core))
            else:
                ends.append((here, 2 * (3 - z) + core))
        pair = swap(saved_inputs, "tensor", middle[0])
        near = lax.ppermute(saved_inputs, "tensor", inner)
        next_near = lax.ppermute(pair, "tensor", inner)
        passed = lax.ppermute(near, "tensor", out_of)
        across = lax.ppermute(saved_inputs, "tensor", ends)
        own = [
            jnp.concatenate([saved_inputs, pair], axis=0),
            add(jnp.concatenate([next_near, near], axis=0), jnp.concatenate([passed, across], axis=0)),
        ]
    else:
        far = swap(saved_inputs, "tensor", top)
        own = [widen(saved_inputs, middle), widen(far, middle)]
    other = [swap(own[0], "tensor", 1), swap(own[1], "tensor", 1)]

    lgs = [grads_of([own[g], other[g]], hidden[g], up_weight, bias, 0, 1) for g in range(2)]
    spreads = [spread("a", lgs[0], dp_bits), spread("t", lgs[1], dp_bits)]

    far_moved = swap(moved, "tensor", top)
    moved_own = [collect(moved, middle), collect(far_moved, middle)]
    moved_other = [[swap(v, "tensor", 1) for v in vs] for vs in moved_own]

    parts = []
    cut = depth // 2
    for start, cols in ((0, cut), (cut, depth - cut)):
        keep, send = inputs_part([[lgs[0]], [lgs[1]]], up_weight, start, cols)
        cur = add(keep, swap(send, "tensor", 1))
        for b in reversed(middle):
            n = cur.shape[1] // 2
            cur = add(cur[:, :n], swap(cur[:, n:], "tensor", b))
        parts.append(add(cur[0], swap(cur[1], "tensor", top)))
    input_grads = jnp.concatenate(parts, axis=1)

    sources, lhs_pieces, buffers, rhs_pieces = [], [], [], []
    for g in range(2):
        at, per = len(sources), len(moved_own[g])
        sources += [own[g], other[g]] + moved_own[g] + moved_other[g]
        base, (group_buffers, where) = len(buffers), spreads[g]
        buffers += group_buffers
        for r in range(replicas):
            rhs_pieces += [(base + b, row, size) for b, row, size in where[r]]
            for core in (0, 1):
                if r == 0:
                    lhs_pieces.append((at + core, 0, own[g].shape[0], True))
                else:
                    i = moved_rel.index(r)
                    for k in range(per):
                        lhs_pieces.append((at + 2 + core * per + k, i * shard, shard, False))
    xt = gather_rows(spot, sources, lhs_pieces)
    out = weights_of(xt, buffers, rhs_pieces, factor)
    return (input_grads, out)


def solution(mesh):
    return jax.shard_map(
        body,
        mesh=mesh,
        in_specs=(P(("dp", "tensor"), None), P("dp", "tensor"), P(None, "tensor"), P("tensor")),
        out_specs=(P(("dp", "tensor"), None), P("dp", "tensor")),
        check_vma=False,
    )
```

```python
import math

import jax
import jax.numpy as jnp
from jax import lax
from jax.experimental import pallas as pl
from jax.experimental.pallas import tpu as pltpu
from jax.sharding import PartitionSpec as P


VMEM_BYTES = 24 * 1024 * 1024

DX_PARTS = 3
DX_TILE = 1024


def slope(pre):
    cdf = 0.5 * (1.0 + lax.erf(pre * 0.7071067811865476))
    pdf = jnp.exp(-0.5 * pre * pre) * 0.3989422804014327
    return cdf + pre * pdf


def tile_of(size, most):
    for tile in (1024, 768, 512, 384, 256, 128):
        if tile <= most and size % tile == 0:
            return tile
    return size


def params():
    return pltpu.CompilerParams(vmem_limit_bytes=VMEM_BYTES)


def cost(flops, nbytes, trans=0):
    return pl.CostEstimate(flops=flops, bytes_accessed=nbytes, transcendentals=trans)


def resident(shape):
    return pl.BlockSpec(shape, lambda j, *_: (0,) * len(shape))


def grads_of(parts, hidden, weight, bias, part, count):
    depth = parts[0].shape[1]
    rows = sum(p.shape[0] for p in parts)
    width = weight.shape[1] // count
    bn = tile_of(width, 512)
    steps = width // bn
    n = len(parts)

    def kernel(*refs):
        x_refs, (h_ref, w_ref, b_ref, o_ref, lhs) = refs[:n], refs[n:]

        @pl.when(pl.program_id(0) == 0)
        def _():
            at = 0
            for ref in x_refs:
                lhs[at : at + ref.shape[0]] = ref[...]
                at += ref.shape[0]

        pre = jnp.dot(lhs[...], w_ref[...], preferred_element_type=jnp.float32) + b_ref[...]
        o_ref[...] = (h_ref[...].astype(jnp.float32) * slope(pre)).astype(jnp.bfloat16)

    return pl.pallas_call(
        kernel,
        grid=(steps,),
        in_specs=[resident(p.shape) for p in parts]
        + [
            pl.BlockSpec((rows, bn), lambda j: (0, j + part * steps)),
            pl.BlockSpec((depth, bn), lambda j: (0, j + part * steps)),
            pl.BlockSpec((1, bn), lambda j: (0, j + part * steps)),
        ],
        out_specs=pl.BlockSpec((rows, bn), lambda j: (0, j)),
        out_shape=jax.ShapeDtypeStruct((rows, width), jnp.bfloat16),
        scratch_shapes=[pltpu.VMEM((rows, depth), jnp.bfloat16)],
        compiler_params=params(),
        cost_estimate=cost(2 * rows * depth * width, 2 * depth * width, rows * width),
    )(*parts, hidden, weight, bias)


def inputs_part(groups, weight, start, cols):
    count = len(groups)
    rows = groups[0][0].shape[0]
    _, full = weight.shape
    bd = tile_of(math.gcd(start, cols), DX_TILE)
    steps = cols // bd
    own = rows // 2
    flat = [a for group in groups for a in group]
    n = len(flat)

    def kernel(*refs):
        lg_refs, (w_ref, keep_ref, send_ref, lhs) = refs[:n], refs[n:]

        @pl.when(pl.program_id(0) == 0)
        def _():
            k = 0
            for g in range(count):
                at = 0
                for a in groups[g]:
                    lhs[g * rows : (g + 1) * rows, at : at + a.shape[1]] = lg_refs[k][...]
                    at += a.shape[1]
                    k += 1

        out = lax.dot_general(
            lhs[...], w_ref[...], (((1,), (1,)), ((), ())), preferred_element_type=jnp.float32
        ).astype(jnp.bfloat16)
        for g in range(count):
            keep_ref[g] = out[g * rows : g * rows + own]
            send_ref[g] = out[g * rows + own : (g + 1) * rows]

    shape = jax.ShapeDtypeStruct((count, own, cols), jnp.bfloat16)
    return pl.pallas_call(
        kernel,
        grid=(steps,),
        in_specs=[resident(a.shape) for a in flat]
        + [pl.BlockSpec((bd, full), lambda j: (j + start // bd, 0))],
        out_specs=[pl.BlockSpec((count, own, bd), lambda j: (0, 0, j))] * 2,
        out_shape=[shape, shape],
        scratch_shapes=[pltpu.VMEM((count * rows, full), jnp.bfloat16)],
        compiler_params=params(),
        cost_estimate=cost(2 * count * rows * full * cols, 2 * full * cols),
    )(*flat, weight)


def weights_of(spot, sources, lhs_pieces, buffers, rhs_pieces, prev, factor):
    tokens = sum(p[2] for p in lhs_pieces)
    rows = min(s.shape[1] for s in sources)
    full = buffers[0].shape[1]
    bn = tile_of(full, 1024)
    n, m = len(buffers), len(sources)
    extra = [] if prev is None else [prev]

    def kernel(spot_ref, *refs):
        lg_refs, src_refs, (o_ref, lhs) = refs[:n], refs[n : n + m], refs[-2:]

        @pl.when(pl.program_id(0) == 0)
        def _():
            at = 0
            for s, row, size in lhs_pieces:
                lhs[at : at + size] = src_refs[s][row : row + size]
                at += size

        rhs = jnp.concatenate([lg_refs[b][row : row + size] for b, row, size in rhs_pieces], axis=0)
        acc = lax.dot_general(lhs[...], rhs, (((0,), (0,)), ((), ())), preferred_element_type=jnp.float32)
        if extra:
            acc = acc + refs[n + m][...].astype(jnp.float32)
        if factor is not None:
            acc = acc * factor
        o_ref[...] = acc.astype(jnp.bfloat16)

    def source_spec(s):
        if s.shape[1] > rows:
            return pl.BlockSpec((s.shape[0], rows), lambda j, spot_ref: (0, spot_ref[0]))
        return resident(s.shape)

    by_columns = lambda j, _: (0, j)
    return pl.pallas_call(
        kernel,
        grid_spec=pltpu.PrefetchScalarGridSpec(
            num_scalar_prefetch=1,
            grid=(full // bn,),
            in_specs=[pl.BlockSpec((b.shape[0], bn), by_columns) for b in buffers]
            + [source_spec(s) for s in sources]
            + [pl.BlockSpec((rows, bn), by_columns) for _ in extra],
            out_specs=pl.BlockSpec((rows, bn), by_columns),
            scratch_shapes=[pltpu.VMEM((tokens, rows), jnp.bfloat16)],
        ),
        out_shape=jax.ShapeDtypeStruct((rows, full), jnp.bfloat16),
        compiler_params=params(),
        cost_estimate=cost(2 * tokens * rows * full, 4 * rows * full),
    )(spot, *buffers, *sources, *extra)


def swap(value, axis, bit):
    n = lax.axis_size(axis)
    return lax.ppermute(value, axis, [(i, i ^ bit) for i in range(n)])


def bits_of(n):
    out, b = [], 1
    while b < n:
        out.append(b)
        b *= 2
    return out


def widen(value, bits):
    for b in bits:
        value = jnp.concatenate([value, swap(value, "tensor", b)], axis=0)
    return value


def collect(value, bits):
    values = [value]
    for b in bits:
        values = values + [swap(v, "tensor", b) for v in values]
    return values


def spread(name, value, bits):
    rows = value.shape[0]
    if len(bits) == 2:
        first, second = bits
        a = swap(value, "dp", first)
        b = swap(value, "dp", second)
        tail = swap(a, "dp", second) if name == "a" else swap(b, "dp", first)
        return [value, a, b, tail], {
            0: [(0, 0, rows)],
            first: [(1, 0, rows)],
            second: [(2, 0, rows)],
            first ^ second: [(3, 0, rows)],
        }
    cur, rel = value, [0]
    got, got_rel = None, []
    for k, b in enumerate(bits):
        if k:
            cur, rel = jnp.concatenate([cur, got], axis=0), rel + got_rel
        got = swap(cur, "dp", b)
        got_rel = [r ^ b for r in rel]
    where = {r: [(0, i * rows, rows)] for i, r in enumerate(rel)}
    where.update({r: [(1, i * rows, rows)] for i, r in enumerate(got_rel)})
    return [cur, got], where


def to_owner(x, bits):
    me = lax.axis_index("dp")
    cur, rel = x[None], [0]
    for b in reversed(bits):
        half = cur.shape[2] // 2
        mine = (me // b) % 2
        send = lax.dynamic_slice_in_dim(cur, (1 - mine) * half, half, 2)
        keep = lax.dynamic_slice_in_dim(cur, mine * half, half, 2)
        cur = jnp.concatenate([keep, swap(send, "dp", b)], axis=0)
        rel = rel + [r ^ b for r in rel]
    return cur[1:].reshape(-1, cur.shape[2]), rel[1:]


def add(a, b):
    return (a.astype(jnp.float32) + b.astype(jnp.float32)).astype(jnp.bfloat16)


def body(saved_inputs, hidden_grads, up_weight, up_bias):
    ranks = lax.axis_size("tensor")
    replicas = lax.axis_size("dp")
    me = lax.axis_index("tensor")
    spot = lax.axis_index("dp").astype(jnp.int32).reshape(1)
    shard, depth = saved_inputs.shape
    full = up_weight.shape[1]
    tokens = hidden_grads.shape[0] * replicas
    factor = float(1.0 / (tokens**0.5))
    bits = bits_of(ranks)
    top, middle = bits[-1], bits[1:-1]
    dp_bits = bits_of(replicas)
    bias = up_bias.reshape(1, full)

    order = [0]
    for b in middle:
        order = order + [r ^ b for r in order]
    hidden = []
    for side in (0, top):
        rel = [c ^ r ^ side for c in (0, 1) for r in order]
        hidden.append(
            jnp.concatenate(
                [lax.dynamic_slice_in_dim(hidden_grads, (me ^ r) * shard, shard, 0) for r in rel], axis=0
            )
        )

    moved, moved_rel = to_owner(saved_inputs, dp_bits)
    if len(middle) == 1:
        ends, inner, out_of = [], [], []
        for z, core in ((z, c) for z in range(4) for c in (0, 1)):
            here = 2 * z + core
            if z in (1, 2):
                inner.append((here, 2 * (3 - z) + core))
                out_of.append((here, 2 * (3 * (z - 1)) + core))
            else:
                ends.append((here, 2 * (3 - z) + core))
        pair = swap(saved_inputs, "tensor", middle[0])
        near = lax.ppermute(saved_inputs, "tensor", inner)
        next_near = lax.ppermute(pair, "tensor", inner)
        passed = lax.ppermute(near, "tensor", out_of)
        across = lax.ppermute(saved_inputs, "tensor", ends)
        own = [
            jnp.concatenate([saved_inputs, pair], axis=0),
            add(jnp.concatenate([next_near, near], axis=0), jnp.concatenate([passed, across], axis=0)),
        ]
    else:
        far = swap(saved_inputs, "tensor", top)
        own = [widen(saved_inputs, middle), widen(far, middle)]
    other = [swap(own[0], "tensor", 1), swap(own[1], "tensor", 1)]

    lgs = [grads_of([own[g], other[g]], hidden[g], up_weight, bias, 0, 1) for g in range(2)]
    spreads = [spread("a", lgs[0], dp_bits), spread("t", lgs[1], dp_bits)]

    far_moved = swap(moved, "tensor", top)
    moved_own = [collect(moved, middle), collect(far_moved, middle)]
    moved_other = [[swap(v, "tensor", 1) for v in vs] for vs in moved_own]

    parts = []
    cols = depth // DX_PARTS
    for part in range(DX_PARTS):
        keep, send = inputs_part([[lgs[0]], [lgs[1]]], up_weight, part * cols, cols)
        cur = add(keep, swap(send, "tensor", 1))
        for b in reversed(middle):
            n = cur.shape[1] // 2
            cur = add(cur[:, :n], swap(cur[:, n:], "tensor", b))
        parts.append(add(cur[0], swap(cur[1], "tensor", top)))
    input_grads = jnp.concatenate(parts, axis=1)

    last_hop = replicas - 1
    out = None
    for chosen, scale in ((range(last_hop), None), (range(last_hop, replicas), factor)):
        sources, lhs_pieces, buffers, rhs_pieces = [], [], [], []

        def index_of(things, thing):
            for k, t in enumerate(things):
                if t is thing:
                    return k
            things.append(thing)
            return len(things) - 1

        for g in range(2):
            group_buffers, where = spreads[g]
            for r in chosen:
                for b, row, size in where[r]:
                    rhs_pieces.append((index_of(buffers, group_buffers[b]), row, size))
                for mine, moved_here in ((own[g], moved_own[g]), (other[g], moved_other[g])):
                    if r == 0:
                        lhs_pieces.append((index_of(sources, mine), 0, mine.shape[0]))
                    else:
                        i = moved_rel.index(r)
                        for v in moved_here:
                            lhs_pieces.append((index_of(sources, v), i * shard, shard))
        out = weights_of(spot, sources, lhs_pieces, buffers, rhs_pieces, out, scale)
    return (input_grads, out)


def solution(mesh):
    return jax.shard_map(
        body,
        mesh=mesh,
        in_specs=(P(("dp", "tensor"), None), P("dp", "tensor"), P(None, "tensor"), P("tensor")),
        out_specs=(P(("dp", "tensor"), None), P("dp", "tensor")),
        check_vma=False,
    )
```
